512 devices in a mesh: inst: 16 (over z), span: 8 (over x, y_lo), chord: 4 (over y_hi, core).
Axes of the slice: x: 4, y: 4 (y_hi: 2, y_lo: 2; y = y_hi * 2 + y_lo), z: 16, core: 2. Of those that a mesh axis runs over, the one named last changes fastest.
Arguments:
- adj_source: float32 [16, 32, 32, 1920], P('inst', 'span', 'chord'), may hold values from -6 to 6
- adj_start: float32 [16, 32, 32, 1920], P('inst', 'span', 'chord'), may hold values from -4 to 4
- tiles: bfloat16 [16, 32, 32, 4, 6, 1920], P('inst', 'span', 'chord'), may hold values from -1.25 to 1.25
- tile_cols: int32 [32, 32, 4], P('span', 'chord'), may hold values from 0 to 8, as said below
- inverse_diag: bfloat16 [16, 32, 32, 6, 1920], P('inst', 'span', 'chord'), as said below
- face_src: int32 [2, 8192], P(None, ('span', 'chord')), may hold values from 0 to 10239, as said below
- face_dst: int32 [2, 8192], P(None, ('span', 'chord')), may hold values from 0 to 10239, as said below
- lag_coef: bfloat16 [16, 72, 8192], P('inst', None, ('span', 'chord')), may hold values from -2.5 to 2.5
Outputs:
- adjoint: float32 [16, 32, 32, 1920], P('inst', 'span', 'chord')
- residual: float32 [16, 32, 32, 1920], P('inst', 'span', 'chord')
The draws below stay inside these ranges and needn't reach their ends.
Inputs may be any that keep to these rules, and one draw needn't show every extreme that they name: `tile_cols`: each block row names code 4 (its own block) once and three distinct other codes; code 3 a + b means the block a - 1 spanwise and b - 1 chordwise away. `face_src`: for each side, the 256 entries of one span and chord group are distinct cell numbers of that group. `face_dst`: for each side, the 256 entries of one span and chord group are distinct cell numbers of that group. `inverse_diag`: diagonal entries of each 6 x 6 block lie in 0.4 to 1.6, off-diagonal entries in -0.35 to 0.35.
All inputs are finite; a program needn't handle non-finite values.
Results may differ from the reference program's by a relative error of at most 0.0003.
Values sent between devices are 32-bit elements; how exact they have to be, the bound alone decides.
No kernel may reach another device: no remote copies, remote signals or barrier semaphores. Data moves between devices by JAX's collectives and lax.ppermute only.
A program may use at most 64 MiB of HBM per device.

```python
import math
import jax
import jax.numpy as jnp
from jax import lax

NV = 6
BLK = 320
K = 4
SB = 4
CB = 8
PF = 256
SWEEPS = 2
NT = 16
LAG = 4
NSB = 32
NCB = 32
CELLS_DEV = 10240
FACES = 8192
N_SPAN = 8
N_CHORD = 4


def draw_inverse_diag(key, part):
    first, second = jax.random.split(key)
    shape = (NT, NSB, NCB, NV, NV, BLK)
    diagonal = jax.random.uniform(first, shape, jnp.float32, 0.5, 1.5)
    coupling = jnp.clip(0.2 * jax.random.normal(second, shape, jnp.float32), -0.35, 0.35)
    same = (jnp.arange(NV)[:, None] == jnp.arange(NV)[None, :])[:, :, None]
    return jnp.where(same, diagonal, coupling).reshape(NT, NSB, NCB, NV, NV * BLK).astype(jnp.bfloat16)


def draw_tile_cols(key, part):
    others = jnp.array([0, 1, 2, 3, 5, 6, 7, 8], dtype=jnp.int32)

    def one_row(row_key):
        pick_key, order_key = jax.random.split(row_key)
        chosen = jax.random.permutation(pick_key, others)[:3]
        slots = jnp.concatenate([chosen, jnp.array([4], dtype=jnp.int32)])
        return jax.random.permutation(order_key, slots)
    return jax.vmap(one_row)(jax.random.split(key, NSB * NCB)).reshape(NSB, NCB, K).astype(jnp.int32)


def face_draw(key):
    groups = FACES // PF

    def one_list(list_key):
        pick_key, order_key = jax.random.split(list_key)
        middle = (jax.random.permutation(pick_key, CELLS_DEV - 2)[:PF - 2] + 1).astype(jnp.int32)
        ends = jnp.array([0, CELLS_DEV - 1], dtype=jnp.int32)
        return jax.random.permutation(order_key, jnp.concatenate([ends, middle])).astype(jnp.int32)
    return jax.vmap(one_list)(jax.random.split(key, 2 * groups)).reshape(2, FACES)


def draw_face_src(key, part):
    return face_draw(jax.random.fold_in(key, 11))


def draw_face_dst(key, part):
    return face_draw(jax.random.fold_in(key, 23))


def levels(stream_key, shape, pieces, low, largest):
    level, own = 1.0, jax.random.fold_in(stream_key, 6)
    for axis_at, shards_of in pieces:
        steps = jnp.exp(jax.random.uniform(jax.random.fold_in(own, axis_at), (shards_of,), jnp.float32, low / len(pieces), largest / len(pieces)))
        level = level * jnp.repeat(steps, shape[axis_at] // shards_of).reshape([-1 if axis == axis_at else 1 for axis in range(len(shape))])
    return level


def centred(rng, dims, scale, reach, cuts=(), held_as=jnp.bfloat16):
    result = scale * jax.random.normal(rng, dims, jnp.float32)
    if cuts:
        result = result * levels(rng, dims, cuts, -0.22, 0.18)
    return jnp.clip(result, -reach, reach).astype(held_as)


def setup_inputs(seed: int = 0) -> dict:
    splits = jax.random.split(jax.random.key(seed), 9)
    adj_source = centred(splits[0], (NT, NSB, NCB, NV * BLK), 1.0, 6.0, ((0, 16), (1, 8), (2, 4)), jnp.float32)
    adj_start = centred(splits[1], (NT, NSB, NCB, NV * BLK), 0.5, 4.0, ((0, 16), (1, 8), (2, 4)), jnp.float32)
    tiles = centred(splits[2], (NT, NSB, NCB, K, NV, NV * BLK), (K * NV) ** -0.5, 1.25, ((0, 16), (1, 8), (2, 4)))
    tile_cols = draw_tile_cols(jax.random.fold_in(splits[8], 71), 0)
    inverse_diag = draw_inverse_diag(jax.random.fold_in(splits[8], 71), 0)
    face_src = draw_face_src(jax.random.fold_in(splits[8], 71), 0)
    face_dst = draw_face_dst(jax.random.fold_in(splits[8], 71), 0)
    lag_coef = centred(splits[7], (NT, 2 * NV * NV, FACES), NV ** -0.5, 2.5, ((0, 16), (2, 32)))
    return dict(adj_source=adj_source, adj_start=adj_start, tiles=tiles, tile_cols=tile_cols, inverse_diag=inverse_diag, face_src=face_src, face_dst=face_dst, lag_coef=lag_coef)


rotor_rate = 0.25
spectral_viscosity = 0.03
highest = lax.Precision.HIGHEST


def spectral_row(instance, total):
    others = jnp.arange(total, dtype=jnp.int32)
    offset = jnp.mod(others - instance, total)
    angle = (math.pi / total) * offset.astype(jnp.float32)
    parity = jnp.where(jnp.mod(offset, 2) == 0, 1.0, -1.0).astype(jnp.float32)
    sine = jnp.where(offset == 0, 1.0, jnp.sin(angle)).astype(jnp.float32)
    first = jnp.where(offset == 0, 0.0, 0.5 * parity * jnp.cos(angle) / sine)
    second = jnp.where(offset == 0, -(total * total + 2) / 12.0, -0.5 * parity / (sine * sine))
    return (rotor_rate * first - spectral_viscosity * second).astype(jnp.float32)


def extend(state):
    wrapped = jnp.concatenate([state[:, -1:], state, state[:, :1]], axis=1)
    return jnp.pad(wrapped, ((1, 1), (0, 0), (0, 0)))


def tile_product(extended, tiles, tile_cols):
    rows = tile_cols.shape[0]
    cols = tile_cols.shape[1]
    width = extended.shape[-1]
    selected = jnp.zeros((rows, cols, tile_cols.shape[2], width), jnp.float32)
    for code in range(9):
        view = extended[code // 3: code // 3 + rows, code % 3: code % 3 + cols]
        selected = selected + jnp.where((tile_cols == code)[..., None], view[:, :, None, :], 0.0)
    cells = width // NV
    coupled = tiles.astype(jnp.float32).reshape(rows, cols, tile_cols.shape[2], NV, NV, cells) * selected.reshape(rows, cols, tile_cols.shape[2], 1, NV, cells)
    return jnp.sum(coupled, axis=(2, 4)).reshape(rows, cols, width)


def lag_pack(blocks, faces):
    return blocks[faces // BLK, :, faces % BLK].T


def lag_apply(pack_behind, pack_ahead, coef, dst_behind, dst_ahead):
    coupling = coef.astype(jnp.float32).reshape(2, NV, NV, PF)
    term = jnp.zeros((SB * CB, NV, BLK), jnp.float32)
    for direction, packed, target in ((0, pack_behind, dst_behind), (1, pack_ahead, dst_ahead)):
        contrib = jnp.sum(coupling[direction] * packed[None, :, :], axis=1)
        term = term.at[target // BLK, :, target % BLK].add(contrib.T)
    return term


def precondition(inverse, residual):
    lead = residual.shape[:-1]
    product = inverse.astype(jnp.float32).reshape(lead + (NV, NV, BLK)) * residual.reshape(lead + (1, NV, BLK))
    return jnp.sum(product, axis=-2).reshape(lead + (NV * BLK,))


def reference(adj_source, adj_start, tiles, tile_cols, inverse_diag, face_src, face_dst, lag_coef):
    groups = N_SPAN * N_CHORD

    def grouped(state):
        return state.reshape(N_SPAN, SB, N_CHORD, CB, NV, BLK).transpose(0, 2, 1, 3, 4, 5).reshape(groups, SB * CB, NV, BLK)

    def ungrouped(blocks):
        return blocks.reshape(N_SPAN, N_CHORD, SB, CB, NV * BLK).transpose(0, 2, 1, 3, 4).reshape(NSB, NCB, NV * BLK)

    src_groups = face_src.reshape(2, groups, PF)
    dst_groups = face_dst.reshape(2, groups, PF)

    def apply_operator(state):
        def one_instance(instance):
            own = state[instance]
            tile_term = tile_product(extend(own), tiles[instance], tile_cols)
            weights = spectral_row(instance, NT)
            spectral_term = jnp.einsum('s,spqf->pqf', weights, state, precision=highest)
            behind = grouped(state[jnp.mod(instance - LAG, NT)])
            ahead = grouped(state[jnp.mod(instance + LAG, NT)])
            pack_behind = jax.vmap(lag_pack)(behind, src_groups[0])
            pack_ahead = jax.vmap(lag_pack)(ahead, src_groups[1])
            coef_groups = lag_coef[instance].reshape(2 * NV * NV, groups, PF).transpose(1, 0, 2)
            lag_term = jax.vmap(lag_apply)(pack_behind, pack_ahead, coef_groups, dst_groups[0], dst_groups[1])
            return tile_term + spectral_term + ungrouped(lag_term)

        return lax.map(one_instance, jnp.arange(NT, dtype=jnp.int32))

    def update_one(pair):
        return precondition(pair[0], pair[1])

    state = adj_start
    residual = adj_source
    for sweep_index in range(SWEEPS):
        residual = adj_source - apply_operator(state)
        state = state + lax.map(update_one, (inverse_diag, residual))
    return state, residual
```

```python
import math

import jax
import jax.numpy as jnp
from jax import lax
from jax.experimental import pallas as pl
from jax.experimental.pallas import tpu as pltpu
from jax.sharding import PartitionSpec as P

NV = 6
BLK = 320
SB = 4
CB = 8
K = 4
PF = 256
SWEEPS = 2
NT = 16
LAG = 4
WIDTH = NV * BLK
LANES = 128
STRIPS = WIDTH // LANES
SHARE = 32
FACE_ROW = SB * STRIPS * 8

rotor_rate = 0.25
spectral_viscosity = 0.03


def spectral_coefficients():
    values = []
    for offset in range(NT):
        parity = 1.0 if offset % 2 == 0 else -1.0
        if offset == 0:
            first, second = 0.0, -(NT * NT + 2) / 12.0
        else:
            angle = math.pi * offset / NT
            first = 0.5 * parity * math.cos(angle) / math.sin(angle)
            second = -0.5 * parity / math.sin(angle) ** 2
        values.append(rotor_rate * first - spectral_viscosity * second)
    return values


def split_cells(cells):
    block = lax.shift_right_logical(cells * 6554, 21)
    return block, cells - block * BLK


def three_parts(value):
    high = value.astype(jnp.bfloat16)
    rest = value - high.astype(jnp.float32)
    middle = rest.astype(jnp.bfloat16)
    low = (rest - middle.astype(jnp.float32)).astype(jnp.bfloat16)
    return high, middle, low


def one_hot(size, row):
    hit = lax.broadcasted_iota(jnp.int32, (size, row.shape[1]), 0) == row
    return jnp.where(hit, 1.0, 0.0).astype(jnp.bfloat16)


def emit_exchange(state_ref, src_ref, send_ref):
    for p in range(SB):
        for strip in range(STRIPS):
            row = (p * STRIPS + strip) * 8
            send_ref[row : row + 8, :] = state_ref[p, :, strip * LANES : (strip + 1) * LANES]
    flat = [
        jnp.concatenate([state_ref[p, :, w * BLK : (w + 1) * BLK] for p in range(SB)], axis=0)
        for w in range(NV)
    ]
    rows = SB * CB
    parts = [three_parts(value) for value in flat]
    stacked = jnp.concatenate([parts[w][n] for n in range(3) for w in range(NV)], axis=0)
    for side in range(2):
        block, cell = split_cells(src_ref[side : side + 1, :])
        picked = jnp.dot(stacked, one_hot(BLK, cell), preferred_element_type=jnp.float32)
        count = NV * rows
        picked = picked[:count] + (picked[count : 2 * count] + picked[2 * count :])
        mine = lax.broadcasted_iota(jnp.int32, (rows, PF), 0) == block
        pack = jnp.concatenate(
            [
                jnp.sum(jnp.where(mine, picked[w * rows : (w + 1) * rows], 0.0), axis=0, keepdims=True)
                for w in range(NV)
            ]
            + [jnp.zeros((8 - NV, PF), jnp.float32)],
            axis=0,
        )
        for half in range(2):
            row = FACE_ROW + side * 16 + half * 8
            send_ref[row : row + 8, :] = pack[:, half * LANES : (half + 1) * LANES]


def emit_edges(state_ref, low_ref, high_ref):
    for p in range(SB):
        low_ref[p : p + 1, :] = state_ref[p, CB - 1 : CB, :]
        high_ref[p : p + 1, :] = state_ref[p, 0:1, :]


def start_kernel(state_ref, src_ref, send_ref):
    emit_exchange(state_ref, src_ref, send_ref)


def spectral_kernel(who_ref, in_ref, out_ref):
    coef = spectral_coefficients()
    half = NT // 2

    @pl.when(who_ref[0] != NT - 1)
    def _():
        for group in range(SHARE // 8):
            rows = slice(group * 8, group * 8 + 8)
            sums = [in_ref[s, rows, :] + in_ref[s + half, rows, :] for s in range(half)]
            gaps = [in_ref[s, rows, :] - in_ref[s + half, rows, :] for s in range(half)]
            for t in range(half):
                even = odd = None
                for s in range(half):
                    near, far = coef[(s - t) % NT], coef[(s - t + half) % NT]
                    one = sums[s] * jnp.float32(0.5 * (near + far))
                    two = gaps[s] * jnp.float32(0.5 * (near - far))
                    even = one if even is None else even + one
                    odd = two if odd is None else odd + two
                out_ref[t, rows, :] = even + odd
                out_ref[t + half, rows, :] = even - odd

    @pl.when(who_ref[0] == NT - 1)
    def _():
        for t in range(NT):
            out_ref[t, 0:16, :] = in_ref[(t - LAG) % NT, 0:16, :]
            out_ref[t, 16:32, :] = in_ref[(t + LAG) % NT, 16:32, :]


def fold(product):
    pair = 2 * BLK
    total = product[:, :pair] + product[:, pair : 2 * pair] + product[:, 2 * pair :]
    return total[:, :BLK] + total[:, BLK:]


def put(ref, row, count, value):
    ref[0, pl.ds(row, count), :] = value[:, :LANES]
    ref[1, pl.ds(row, count), :] = value[:, LANES : 2 * LANES]
    ref[2, pl.ds(row, count), 0 : BLK - 2 * LANES] = value[:, 2 * LANES :]


def take(ref, row):
    parts = [ref[n, pl.ds(row, CB, stride=8), :] for n in range(3)]
    return jnp.concatenate(parts, axis=1)[:, :BLK]


def tile_kernel(
    cols_ref, tiles_ref, state_ref, left_ref, right_ref, below_ref, above_ref, source_ref, out_ref, wide, term
):
    p = pl.program_id(0)

    @pl.when(p == 0)
    def _():
        wide[0:10, :] = below_ref[...]
        wide[(SB + 1) * 16 : (SB + 1) * 16 + 10, :] = above_ref[...]
        for row in range(SB):
            base = (row + 1) * 16
            wide[base : base + 8, :] = state_ref[row]
            wide[base + 8 : base + 9, :] = left_ref[row : row + 1, :]
            wide[base + 9 : base + 10, :] = right_ref[row : row + 1, :]

    def block(q, carry):
        total = None
        for k in range(K):
            code = cols_ref[p, q, k]
            a = lax.div(code, 3)
            side = q + code - 3 * a - 1
            column = jnp.where(side < 0, CB, jnp.where(side == CB, CB + 1, side))
            row = (p + a) * 16 + column
            product = tiles_ref[0, q, k].astype(jnp.float32) * wide[pl.ds(row, 1), :]
            total = product if total is None else total + product
        put(term, pl.multiple_of(q * 8, 8), NV, fold(total))
        return carry

    lax.fori_loop(0, CB, block, 0)
    for v in range(NV):
        lanes = slice(v * BLK, (v + 1) * BLK)
        out_ref[0, :, lanes] = source_ref[0, :, lanes] - take(term, v)


def finish(base_ref, spectral_ref, state_ref, inverse_ref, coef_ref, dst_ref, residual_ref, next_ref, lagged, term):
    coef = coef_ref[...].astype(jnp.float32)
    spread, cells = [], []
    for side in range(2):
        row = FACE_ROW + side * 16
        pack = jnp.concatenate([spectral_ref[row : row + NV, :], spectral_ref[row + 8 : row + 8 + NV, :]], axis=1)
        contrib = []
        for v in range(NV):
            at = (side * NV + v) * NV
            contrib.append(jnp.sum(coef[at : at + NV] * pack, axis=0, keepdims=True))
        contrib = jnp.concatenate(contrib + [jnp.zeros((8 - NV, PF), jnp.float32)], axis=0)
        block, cell = split_cells(dst_ref[side : side + 1, :])
        spread.append(
            jnp.concatenate([jnp.where(block == b, contrib, 0.0) for b in range(SB * CB)], axis=0)
        )
        cells.append(one_hot(BLK, cell))
    stacked = jnp.concatenate(three_parts(jnp.concatenate(spread, axis=1)), axis=0)
    placed = lax.dot_general(
        stacked,
        jnp.concatenate(cells, axis=1),
        (((1,), (1,)), ((), ())),
        preferred_element_type=jnp.float32,
    )
    count = SB * CB * 8
    put(lagged, 0, count, placed[:count] + (placed[count : 2 * count] + placed[2 * count :]))
    for p in range(SB):
        first = p * STRIPS * 8
        spectral = jnp.concatenate(
            [spectral_ref[first + 8 * n : first + 8 * n + 8, :] for n in range(STRIPS)], axis=1
        )
        residual_ref[p] = base_ref[p] - spectral
        for v in range(NV):
            lanes = slice(v * BLK, (v + 1) * BLK)
            residual_ref[p, :, lanes] = (
                residual_ref[p, :, lanes] - take(lagged, p * CB * 8 + v)
            )

        def block(q, carry):
            product = inverse_ref[p, q].astype(jnp.float32) * residual_ref[p, pl.ds(q, 1), :]
            put(term, pl.multiple_of(q * 8, 8), NV, fold(product))
            return carry

        lax.fori_loop(0, CB, block, 0, unroll=True)
        for v in range(NV):
            lanes = slice(v * BLK, (v + 1) * BLK)
            next_ref[p, :, lanes] = state_ref[p, :, lanes] + take(term, v)


def middle_kernel(
    base_ref, spectral_ref, state_ref, inverse_ref, coef_ref, dst_ref, src_ref, next_ref, send_ref, low_ref, high_ref, residual_ref, lagged, term
):
    finish(base_ref, spectral_ref, state_ref, inverse_ref, coef_ref, dst_ref, residual_ref, next_ref, lagged, term)
    emit_exchange(next_ref, src_ref, send_ref)
    emit_edges(next_ref, low_ref, high_ref)


def last_kernel(
    base_ref, spectral_ref, state_ref, inverse_ref, coef_ref, dst_ref, next_ref, residual_ref, lagged, term
):
    finish(base_ref, spectral_ref, state_ref, inverse_ref, coef_ref, dst_ref, residual_ref, next_ref, lagged, term)


def f32(*shape):
    return jax.ShapeDtypeStruct(shape, jnp.float32)


STATE = f32(SB, CB, WIDTH)
EDGE = f32(SB, WIDTH)
SEND = f32(NT * SHARE, LANES)
FINISH_SCRATCH = [pltpu.VMEM((3, SB * CB * 8, LANES), jnp.float32), pltpu.VMEM((3, CB * 8, LANES), jnp.float32)]
ROOM = pltpu.CompilerParams(vmem_limit_bytes=32 << 20)


def start_call(state, src):
    return pl.pallas_call(start_kernel, out_shape=SEND, compiler_params=ROOM)(state, src)


def spectral_call(who, received):
    return pl.pallas_call(
        spectral_kernel,
        out_shape=f32(NT, SHARE, LANES),
        in_specs=[pl.BlockSpec(memory_space=pltpu.SMEM), pl.BlockSpec(memory_space=pltpu.VMEM)],
        compiler_params=ROOM,
    )(who, received)


def tile_call(cols, tiles, state, left, right, below, above, source):
    whole = lambda array: pl.BlockSpec(array.shape, lambda p: (0,) * array.ndim)
    return pl.pallas_call(
        tile_kernel,
        out_shape=STATE,
        grid=(SB,),
        in_specs=[
            pl.BlockSpec(memory_space=pltpu.SMEM),
            pl.BlockSpec((1, CB, K, NV, WIDTH), lambda p: (p, 0, 0, 0, 0)),
            whole(state),
            whole(left),
            whole(right),
            whole(below),
            whole(above),
            pl.BlockSpec((1, CB, WIDTH), lambda p: (p, 0, 0)),
        ],
        out_specs=pl.BlockSpec((1, CB, WIDTH), lambda p: (p, 0, 0)),
        scratch_shapes=[
            pltpu.VMEM(((SB + 2) * 16, WIDTH), jnp.float32),
            pltpu.VMEM((3, CB * 8, LANES), jnp.float32),
        ],
        compiler_params=ROOM,
    )(cols, tiles, state, left, right, below, above, source)


def middle_call(base, spectral, state, inverse, coef, dst, src):
    return pl.pallas_call(
        middle_kernel,
        out_shape=(STATE, SEND, EDGE, EDGE),
        scratch_shapes=[pltpu.VMEM((SB, CB, WIDTH), jnp.float32)] + FINISH_SCRATCH,
        compiler_params=ROOM,
    )(base, spectral, state, inverse, coef, dst, src)


def last_call(base, spectral, state, inverse, coef, dst):
    return pl.pallas_call(
        last_kernel,
        out_shape=(STATE, STATE),
        scratch_shapes=FINISH_SCRATCH,
        compiler_params=ROOM,
    )(base, spectral, state, inverse, coef, dst)


def exchange(array):
    return lax.all_to_all(array, "inst", 0, 0, tiled=True)


def halos(state, low_edge, high_edge):
    n = lax.axis_size("chord")
    left = lax.ppermute(low_edge, "chord", [(i, (i + 1) % n) for i in range(n)])
    right = lax.ppermute(high_edge, "chord", [(i, (i - 1) % n) for i in range(n)])
    n = lax.axis_size("span")
    last = jnp.concatenate([state[SB - 1], left[SB - 1 :], right[SB - 1 :]], axis=0)
    first = jnp.concatenate([state[0], left[:1], right[:1]], axis=0)
    below = lax.ppermute(last, "span", [(i, i + 1) for i in range(n - 1)])
    above = lax.ppermute(first, "span", [(i + 1, i) for i in range(n - 1)])
    return left, right, below, above


def per_device(adj_source, adj_start, tiles, tile_cols, inverse_diag, face_src, face_dst, lag_coef):
    source, state = adj_source[0], adj_start[0]
    tiles, inverse, coef = tiles[0], inverse_diag[0], lag_coef[0]
    who = lax.axis_index("inst").astype(jnp.int32)[None]
    send = start_call(state, face_src)
    low_edge, high_edge = state[:, CB - 1], state[:, 0]
    for sweep in range(SWEEPS):
        received = exchange(send.reshape(NT, SHARE, LANES))
        left, right, below, above = halos(state, low_edge, high_edge)
        spectral = exchange(spectral_call(who, received)).reshape(NT * SHARE, LANES)
        base = tile_call(tile_cols, tiles, state, left, right, below, above, source)
        if sweep < SWEEPS - 1:
            state, send, low_edge, high_edge = middle_call(
                base, spectral, state, inverse, coef, face_dst, face_src
            )
        else:
            state, residual = last_call(base, spectral, state, inverse, coef, face_dst)
    return state[None], residual[None]


def solution(mesh):
    return jax.shard_map(
        per_device,
        mesh=mesh,
        in_specs=(
            P("inst", "span", "chord", None),
            P("inst", "span", "chord", None),
            P("inst", "span", "chord", None, None, None),
            P("span", "chord", None),
            P("inst", "span", "chord", None, None),
            P(None, ("span", "chord")),
            P(None, ("span", "chord")),
            P("inst", None, ("span", "chord")),
        ),
        out_specs=(P("inst", "span", "chord", None), P("inst", "span", "chord", None)),
        check_vma=False,
    )
```

```python
import math

import jax
import jax.numpy as jnp
from jax import lax
from jax.experimental import pallas as pl
from jax.experimental.pallas import tpu as pltpu
from jax.sharding import PartitionSpec as P

NV = 6
BLK = 320
SB = 4
CB = 8
K = 4
PF = 256
SWEEPS = 2
NT = 16
LAG = 4
WIDTH = NV * BLK
LANES = 128
STRIPS = WIDTH // LANES
SHARE = 32
FACE_ROW = SB * STRIPS * 8

rotor_rate = 0.25
spectral_viscosity = 0.03


def spectral_coefficients():
    values = []
    for offset in range(NT):
        parity = 1.0 if offset % 2 == 0 else -1.0
        if offset == 0:
            first, second = 0.0, -(NT * NT + 2) / 12.0
        else:
            angle = math.pi * offset / NT
            first = 0.5 * parity * math.cos(angle) / math.sin(angle)
            second = -0.5 * parity / math.sin(angle) ** 2
        values.append(rotor_rate * first - spectral_viscosity * second)
    return values


def split_cells(cells):
    block = lax.shift_right_logical(cells * 6554, 21)
    return block, cells - block * BLK


def three_parts(value):
    high = value.astype(jnp.bfloat16)
    rest = value - high.astype(jnp.float32)
    middle = rest.astype(jnp.bfloat16)
    low = (rest - middle.astype(jnp.float32)).astype(jnp.bfloat16)
    return high, middle, low


def one_hot(size, row):
    hit = lax.broadcasted_iota(jnp.int32, (size, row.shape[1]), 0) == row
    return jnp.where(hit, 1.0, 0.0).astype(jnp.bfloat16)


def emit_exchange(state_ref, src_ref, send_ref):
    for p in range(SB):
        for strip in range(STRIPS):
            row = (p * STRIPS + strip) * 8
            send_ref[row : row + 8, :] = state_ref[p, :, strip * LANES : (strip + 1) * LANES]
    flat = [
        jnp.concatenate([state_ref[p, :, w * BLK : (w + 1) * BLK] for p in range(SB)], axis=0)
        for w in range(NV)
    ]
    rows = SB * CB
    parts = [three_parts(value) for value in flat]
    stacked = jnp.concatenate([parts[w][n] for n in range(3) for w in range(NV)], axis=0)
    for side in range(2):
        block, cell = split_cells(src_ref[side : side + 1, :])
        picked = jnp.dot(stacked, one_hot(BLK, cell), preferred_element_type=jnp.float32)
        count = NV * rows
        picked = picked[:count] + (picked[count : 2 * count] + picked[2 * count :])
        mine = lax.broadcasted_iota(jnp.int32, (rows, PF), 0) == block
        pack = jnp.concatenate(
            [
                jnp.sum(jnp.where(mine, picked[w * rows : (w + 1) * rows], 0.0), axis=0, keepdims=True)
                for w in range(NV)
            ]
            + [jnp.zeros((8 - NV, PF), jnp.float32)],
            axis=0,
        )
        for half in range(2):
            row = FACE_ROW + side * 16 + half * 8
            send_ref[row : row + 8, :] = pack[:, half * LANES : (half + 1) * LANES]


def emit_edges(state_ref, low_ref, high_ref):
    for p in range(SB):
        low_ref[p : p + 1, :] = state_ref[p, CB - 1 : CB, :]
        high_ref[p : p + 1, :] = state_ref[p, 0:1, :]


def start_kernel(state_ref, src_ref, send_ref, low_ref, high_ref, state, src, sems):
    copies = [
        pltpu.make_async_copy(state_ref, state, sems.at[0]),
        pltpu.make_async_copy(src_ref, src, sems.at[1]),
    ]
    for copy in copies:
        copy.start()
    for copy in copies:
        copy.wait()
    emit_exchange(state, src, send_ref)
    emit_edges(state, low_ref, high_ref)


def spectral_kernel(who_ref, in_ref, out_ref):
    coef = spectral_coefficients()
    half = NT // 2

    @pl.when(who_ref[0] != NT - 1)
    def _():
        for group in range(SHARE // 8):
            rows = slice(group * 8, group * 8 + 8)
            sums = [in_ref[s, rows, :] + in_ref[s + half, rows, :] for s in range(half)]
            gaps = [in_ref[s, rows, :] - in_ref[s + half, rows, :] for s in range(half)]
            for t in range(half):
                even = odd = None
                for s in range(half):
                    near, far = coef[(s - t) % NT], coef[(s - t + half) % NT]
                    one = sums[s] * jnp.float32(0.5 * (near + far))
                    two = gaps[s] * jnp.float32(0.5 * (near - far))
                    even = one if even is None else even + one
                    odd = two if odd is None else odd + two
                out_ref[t, rows, :] = even + odd
                out_ref[t + half, rows, :] = even - odd

    @pl.when(who_ref[0] == NT - 1)
    def _():
        for t in range(NT):
            out_ref[t, 0:16, :] = in_ref[(t - LAG) % NT, 0:16, :]
            out_ref[t, 16:32, :] = in_ref[(t + LAG) % NT, 16:32, :]


def put(ref, row, count, value):
    ref[0, pl.ds(row, count), :] = value[:, :LANES]
    ref[1, pl.ds(row, count), :] = value[:, LANES : 2 * LANES]
    ref[2, pl.ds(row, count), 0 : BLK - 2 * LANES] = value[:, 2 * LANES :]


def take(ref, row):
    parts = [ref[n, pl.ds(row, CB, stride=8), :] for n in range(3)]
    return jnp.concatenate(parts, axis=1)[:, :BLK]


def fold_pair(total):
    return total[:, :BLK] + total[:, BLK:]


def sum_pairs(product):
    pair = 2 * BLK
    return product[:, :pair] + product[:, pair : 2 * pair] + product[:, 2 * pair :]


def tile_kernel(
    cols_ref, tiles_hbm, state_ref, left_ref, right_ref, below_ref, above_ref, source_ref, out_ref, tiles_ref, wide, chosen, partial, sems
):
    def fetch(p):
        return pltpu.make_async_copy(tiles_hbm.at[p], tiles_ref.at[p], sems.at[p])

    for p in range(SB):
        fetch(p).start()
    wide[0:10, :] = below_ref[...]
    wide[(SB + 1) * 16 : (SB + 1) * 16 + 10, :] = above_ref[...]
    for row in range(SB):
        base = (row + 1) * 16
        wide[base : base + 8, :] = state_ref[row]
        wide[base + 8 : base + 9, :] = left_ref[row : row + 1, :]
        wide[base + 9 : base + 10, :] = right_ref[row : row + 1, :]

    def block_row(p, carry):
        fetch(p).wait()
        for q in range(CB):
            for k in range(K):
                code = cols_ref[p, k, q]
                a = lax.shift_right_logical(code * 11, 5)
                side = q + code - 3 * a - 1
                column = jnp.where(side < 0, CB, jnp.where(side == CB, CB + 1, side))
                row = (p + a) * 16 + column
                chosen[q * 8 + k : q * 8 + k + 1, :] = wide[pl.ds(row, 1), :]
            inputs = chosen[q * 8 : q * 8 + K, :]
            for v in range(NV):
                total = sum_pairs(tiles_ref[p, q, v].astype(jnp.float32) * inputs)
                for n in range(2 * BLK // LANES):
                    at = v * CB * K + q * K
                    partial[n, at : at + K, :] = total[:, n * LANES : (n + 1) * LANES]
        for v in range(NV):
            lanes = slice(v * BLK, (v + 1) * BLK)
            total = None
            for k in range(K):
                rows = pl.ds(v * CB * K + k, CB, stride=K)
                one = jnp.concatenate([partial[n, rows, :] for n in range(2 * BLK // LANES)], axis=1)
                total = one if total is None else total + one
            out_ref[p, :, lanes] = source_ref[p, :, lanes] - fold_pair(total)
        return carry

    lax.fori_loop(0, SB, block_row, 0)


def finish(base_ref, spectral_ref, state_ref, inverse_hbm, coef_ref, dst_ref, residual_ref, next_ref, lagged, inverse_ref, sem):
    fetch = pltpu.make_async_copy(inverse_hbm, inverse_ref, sem)
    fetch.start()
    coef = coef_ref[...].astype(jnp.float32)
    spread, cells = [], []
    for side in range(2):
        row = FACE_ROW + side * 16
        pack = jnp.concatenate([spectral_ref[row : row + NV, :], spectral_ref[row + 8 : row + 8 + NV, :]], axis=1)
        contrib = []
        for v in range(NV):
            at = (side * NV + v) * NV
            contrib.append(jnp.sum(coef[at : at + NV] * pack, axis=0, keepdims=True))
        contrib = jnp.concatenate(contrib + [jnp.zeros((8 - NV, PF), jnp.float32)], axis=0)
        block, cell = split_cells(dst_ref[side : side + 1, :])
        spread.append(
            jnp.concatenate([jnp.where(block == b, contrib, 0.0) for b in range(SB * CB)], axis=0)
        )
        cells.append(one_hot(BLK, cell))
    stacked = jnp.concatenate(three_parts(jnp.concatenate(spread, axis=1)), axis=0)
    placed = lax.dot_general(
        stacked,
        jnp.concatenate(cells, axis=1),
        (((1,), (1,)), ((), ())),
        preferred_element_type=jnp.float32,
    )
    count = SB * CB * 8
    put(lagged, 0, count, placed[:count] + (placed[count : 2 * count] + placed[2 * count :]))
    fetch.wait()
    for p in range(SB):
        first = p * STRIPS * 8
        spectral = jnp.concatenate(
            [spectral_ref[first + 8 * n : first + 8 * n + 8, :] for n in range(STRIPS)], axis=1
        )
        residual_ref[p] = base_ref[p] - spectral
        for v in range(NV):
            lanes = slice(v * BLK, (v + 1) * BLK)
            residual_ref[p, :, lanes] = (
                residual_ref[p, :, lanes] - take(lagged, p * CB * 8 + v)
            )

        for v in range(NV):
            lanes = slice(v * BLK, (v + 1) * BLK)
            product = inverse_ref[p, v].astype(jnp.float32) * residual_ref[p]
            next_ref[p, :, lanes] = state_ref[p, :, lanes] + fold_pair(sum_pairs(product))


def middle_kernel(
    base_ref, spectral_ref, state_ref, inverse_hbm, coef_ref, dst_ref, src_ref, next_ref, send_ref, low_ref, high_ref, residual_ref, lagged, inverse, sem
):
    finish(base_ref, spectral_ref, state_ref, inverse_hbm, coef_ref, dst_ref, residual_ref, next_ref, lagged, inverse, sem)
    emit_exchange(next_ref, src_ref, send_ref)
    emit_edges(next_ref, low_ref, high_ref)


def last_kernel(
    base_ref, spectral_ref, state_ref, inverse_hbm, coef_ref, dst_ref, next_ref, residual_ref, lagged, inverse, sem
):
    finish(base_ref, spectral_ref, state_ref, inverse_hbm, coef_ref, dst_ref, residual_ref, next_ref, lagged, inverse, sem)


def f32(*shape):
    return jax.ShapeDtypeStruct(shape, jnp.float32)


STATE = f32(SB, CB, WIDTH)
EDGE = f32(SB, WIDTH)
SEND = f32(NT * SHARE, LANES)
FINISH_SCRATCH = [
    pltpu.VMEM((3, SB * CB * 8, LANES), jnp.float32),
    pltpu.VMEM((SB, NV, CB, WIDTH), jnp.bfloat16),
    pltpu.SemaphoreType.DMA,
]
def room(mebibytes):
    return pltpu.CompilerParams(vmem_limit_bytes=mebibytes << 20)


def in_hbm(array):
    return pltpu.with_memory_space_constraint(array, pltpu.HBM)


def start_call(state, src):
    return pl.pallas_call(
        start_kernel,
        out_shape=(SEND, EDGE, EDGE),
        in_specs=[pl.BlockSpec(memory_space=pltpu.HBM)] * 2,
        scratch_shapes=[
            pltpu.VMEM(state.shape, state.dtype),
            pltpu.VMEM(src.shape, src.dtype),
            pltpu.SemaphoreType.DMA((2,)),
        ],
        compiler_params=room(8),
    )(in_hbm(state), in_hbm(src))


def spectral_call(who, received):
    return pl.pallas_call(
        spectral_kernel,
        out_shape=f32(NT, SHARE, LANES),
        in_specs=[pl.BlockSpec(memory_space=pltpu.SMEM), pl.BlockSpec(memory_space=pltpu.VMEM)],
        compiler_params=room(4),
    )(who, received)


def tile_call(cols, tiles, state, left, right, below, above, source):
    in_vmem = pl.BlockSpec(memory_space=pltpu.VMEM)
    return pl.pallas_call(
        tile_kernel,
        out_shape=STATE,
        in_specs=[pl.BlockSpec(memory_space=pltpu.SMEM), pl.BlockSpec(memory_space=pltpu.HBM)] + [in_vmem] * 6,
        scratch_shapes=[
            pltpu.VMEM(tiles.shape, tiles.dtype),
            pltpu.VMEM(((SB + 2) * 16, WIDTH), jnp.float32),
            pltpu.VMEM((CB * 8, WIDTH), jnp.float32),
            pltpu.VMEM((2 * BLK // LANES, NV * CB * K, LANES), jnp.float32),
            pltpu.SemaphoreType.DMA((SB,)),
        ],
        compiler_params=room(8),
    )(cols, in_hbm(tiles), state, left, right, below, above, source)


def finish_specs(count):
    specs = [pl.BlockSpec(memory_space=pltpu.VMEM)] * count
    specs[3] = pl.BlockSpec(memory_space=pltpu.HBM)
    return specs


def middle_call(base, spectral, state, inverse, coef, dst, src):
    return pl.pallas_call(
        middle_kernel,
        out_shape=(STATE, SEND, EDGE, EDGE),
        in_specs=finish_specs(7),
        scratch_shapes=[pltpu.VMEM((SB, CB, WIDTH), jnp.float32)] + FINISH_SCRATCH,
        compiler_params=room(8),
    )(base, spectral, state, in_hbm(inverse), coef, dst, src)


def last_call(base, spectral, state, inverse, coef, dst):
    return pl.pallas_call(
        last_kernel,
        out_shape=(STATE, STATE),
        in_specs=finish_specs(6),
        scratch_shapes=FINISH_SCRATCH,
        compiler_params=room(8),
    )(base, spectral, state, in_hbm(inverse), coef, dst)


def exchange(array):
    return lax.all_to_all(array, "inst", 0, 0, tiled=True)


def halos(state, low_edge, high_edge):
    n = lax.axis_size("chord")
    left = lax.ppermute(low_edge, "chord", [(i, (i + 1) % n) for i in range(n)])
    right = lax.ppermute(high_edge, "chord", [(i, (i - 1) % n) for i in range(n)])
    n = lax.axis_size("span")
    last = jnp.concatenate([state[SB - 1], left[SB - 1 :], right[SB - 1 :]], axis=0)
    first = jnp.concatenate([state[0], left[:1], right[:1]], axis=0)
    below = lax.ppermute(last, "span", [(i, i + 1) for i in range(n - 1)])
    above = lax.ppermute(first, "span", [(i + 1, i) for i in range(n - 1)])
    return left, right, below, above


def per_device(adj_source, adj_start, tiles, tile_cols, inverse_diag, face_src, face_dst, lag_coef):
    source, state = adj_source[0], adj_start[0]
    tiles = tiles[0].transpose(0, 1, 3, 2, 4)
    inverse = inverse_diag[0].transpose(0, 2, 1, 3)
    tile_cols = tile_cols.transpose(0, 2, 1)
    coef = lag_coef[0]
    who = lax.axis_index("inst").astype(jnp.int32)[None]
    send, low_edge, high_edge = start_call(state, face_src)
    for sweep in range(SWEEPS):
        received = exchange(send.reshape(NT, SHARE, LANES))
        left, right, below, above = halos(state, low_edge, high_edge)
        spectral = exchange(spectral_call(who, received)).reshape(NT * SHARE, LANES)
        base = tile_call(tile_cols, tiles, state, left, right, below, above, source)
        if sweep < SWEEPS - 1:
            state, send, low_edge, high_edge = middle_call(
                base, spectral, state, inverse, coef, face_dst, face_src
            )
        else:
            state, residual = last_call(base, spectral, state, inverse, coef, face_dst)
    return state[None], residual[None]


def solution(mesh):
    return jax.shard_map(
        per_device,
        mesh=mesh,
        in_specs=(
            P("inst", "span", "chord", None),
            P("inst", "span", "chord", None),
            P("inst", "span", "chord", None, None, None),
            P("span", "chord", None),
            P("inst", "span", "chord", None, None),
            P(None, ("span", "chord")),
            P(None, ("span", "chord")),
            P("inst", None, ("span", "chord")),
        ),
        out_specs=(P("inst", "span", "chord", None), P("inst", "span", "chord", None)),
        check_vma=False,
    )
```

```python
import math

import jax
import jax.numpy as jnp
from jax import lax
from jax.experimental import pallas as pl
from jax.experimental.pallas import tpu as pltpu
from jax.sharding import PartitionSpec as P

NV = 6
BLK = 320
SB = 4
CB = 8
K = 4
PF = 256
SWEEPS = 2
NT = 16
LAG = 4
WIDTH = NV * BLK
LANES = 128
STRIPS = WIDTH // LANES
SHARE = 32
FACE_ROW = SB * STRIPS * 8

rotor_rate = 0.25
spectral_viscosity = 0.03


def spectral_coefficients():
    values = []
    for offset in range(NT):
        parity = 1.0 if offset % 2 == 0 else -1.0
        if offset == 0:
            first, second = 0.0, -(NT * NT + 2) / 12.0
        else:
            angle = math.pi * offset / NT
            first = 0.5 * parity * math.cos(angle) / math.sin(angle)
            second = -0.5 * parity / math.sin(angle) ** 2
        values.append(rotor_rate * first - spectral_viscosity * second)
    return values


def split_cells(cells):
    block = lax.shift_right_logical(cells * 6554, 21)
    return block, cells - block * BLK


def three_parts(value):
    high = value.astype(jnp.bfloat16)
    rest = value - high.astype(jnp.float32)
    middle = rest.astype(jnp.bfloat16)
    low = (rest - middle.astype(jnp.float32)).astype(jnp.bfloat16)
    return high, middle, low


def one_hot(size, row):
    hit = lax.broadcasted_iota(jnp.int32, (size, row.shape[1]), 0) == row
    return jnp.where(hit, 1.0, 0.0).astype(jnp.bfloat16)


def emit_exchange(state_ref, src_ref, send_ref):
    for p in range(SB):
        for strip in range(STRIPS):
            row = (p * STRIPS + strip) * 8
            send_ref[row : row + 8, :] = state_ref[p, :, strip * LANES : (strip + 1) * LANES]
    flat = [
        jnp.concatenate([state_ref[p, :, w * BLK : (w + 1) * BLK] for p in range(SB)], axis=0)
        for w in range(NV)
    ]
    rows = SB * CB
    parts = [three_parts(value) for value in flat]
    stacked = jnp.concatenate([parts[w][n] for n in range(3) for w in range(NV)], axis=0)
    for side in range(2):
        block, cell = split_cells(src_ref[side : side + 1, :])
        picked = jnp.dot(stacked, one_hot(BLK, cell), preferred_element_type=jnp.float32)
        count = NV * rows
        picked = picked[:count] + (picked[count : 2 * count] + picked[2 * count :])
        mine = lax.broadcasted_iota(jnp.int32, (rows, PF), 0) == block
        pack = jnp.concatenate(
            [
                jnp.sum(jnp.where(mine, picked[w * rows : (w + 1) * rows], 0.0), axis=0, keepdims=True)
                for w in range(NV)
            ]
            + [jnp.zeros((8 - NV, PF), jnp.float32)],
            axis=0,
        )
        for half in range(2):
            row = FACE_ROW + side * 16 + half * 8
            send_ref[row : row + 8, :] = pack[:, half * LANES : (half + 1) * LANES]


def emit_edges(state_ref, low_ref, high_ref):
    for p in range(SB):
        low_ref[p : p + 1, :] = state_ref[p, CB - 1 : CB, :]
        high_ref[p : p + 1, :] = state_ref[p, 0:1, :]


def start_kernel(state_ref, src_ref, send_ref, low_ref, high_ref, state, src, sems):
    copies = [
        pltpu.make_async_copy(state_ref, state, sems.at[0]),
        pltpu.make_async_copy(src_ref, src, sems.at[1]),
    ]
    for copy in copies:
        copy.start()
    for copy in copies:
        copy.wait()
    emit_exchange(state, src, send_ref)
    emit_edges(state, low_ref, high_ref)


def spectral_kernel(who_ref, in_ref, out_ref):
    coef = spectral_coefficients()
    half = NT // 2

    @pl.when(who_ref[0] != NT - 1)
    def _():
        for group in range(SHARE // 8):
            rows = slice(group * 8, group * 8 + 8)
            sums = [in_ref[s, rows, :] + in_ref[s + half, rows, :] for s in range(half)]
            gaps = [in_ref[s, rows, :] - in_ref[s + half, rows, :] for s in range(half)]
            for t in range(half):
                even = odd = None
                for s in range(half):
                    near, far = coef[(s - t) % NT], coef[(s - t + half) % NT]
                    one = sums[s] * jnp.float32(0.5 * (near + far))
                    two = gaps[s] * jnp.float32(0.5 * (near - far))
                    even = one if even is None else even + one
                    odd = two if odd is None else odd + two
                out_ref[t, rows, :] = even + odd
                out_ref[t + half, rows, :] = even - odd

    @pl.when(who_ref[0] == NT - 1)
    def _():
        for t in range(NT):
            out_ref[t, 0:16, :] = in_ref[(t - LAG) % NT, 0:16, :]
            out_ref[t, 16:32, :] = in_ref[(t + LAG) % NT, 16:32, :]


def put(ref, row, count, value):
    ref[0, pl.ds(row, count), :] = value[:, :LANES]
    ref[1, pl.ds(row, count), :] = value[:, LANES : 2 * LANES]
    ref[2, pl.ds(row, count), 0 : BLK - 2 * LANES] = value[:, 2 * LANES :]


def take(ref, row):
    parts = [ref[n, pl.ds(row, CB, stride=8), :] for n in range(3)]
    return jnp.concatenate(parts, axis=1)[:, :BLK]


def fold_pair(total):
    return total[:, :BLK] + total[:, BLK:]


def sum_pairs(product):
    pair = 2 * BLK
    return product[:, :pair] + product[:, pair : 2 * pair] + product[:, 2 * pair :]


def tile_kernel(
    cols_hbm, tiles_hbm, state_ref, left_ref, right_ref, below_ref, above_ref, source_hbm, out_ref, cols_ref, tiles_ref, source_ref, wide, chosen, partial, sems, tile_sems
):
    def fetch(p):
        return pltpu.make_async_copy(tiles_hbm.at[p], tiles_ref.at[p], tile_sems.at[p])

    copies = [pltpu.make_async_copy(cols_hbm, cols_ref, sems.at[0])]
    for row in range(SB):
        base = (row + 1) * 16
        copies.append(
            pltpu.make_async_copy(state_ref.at[row], wide.at[pl.ds(base, CB)], sems.at[row + 1])
        )
    late = pltpu.make_async_copy(source_hbm, source_ref, sems.at[SB + 1])
    for copy in copies:
        copy.start()
    for p in range(SB):
        fetch(p).start()
    late.start()
    wide[0:CB, :] = below_ref[...]
    wide[(SB + 1) * 16 : (SB + 1) * 16 + CB, :] = above_ref[...]
    for row, base in enumerate([16, 32, 48, 64, 0, (SB + 1) * 16]):
        wide[base + 8 : base + 9, :] = left_ref[row : row + 1, :]
        wide[base + 9 : base + 10, :] = right_ref[row : row + 1, :]
    for copy in copies:
        copy.wait()
    late.wait()

    def block_row(p, carry):
        fetch(p).wait()
        for q in range(CB):
            for k in range(K):
                code = cols_ref[p, k, q]
                a = lax.shift_right_logical(code * 11, 5)
                side = q + code - 3 * a - 1
                column = jnp.where(side < 0, CB, jnp.where(side == CB, CB + 1, side))
                row = (p + a) * 16 + column
                chosen[q * 8 + k : q * 8 + k + 1, :] = wide[pl.ds(row, 1), :]
            inputs = chosen[q * 8 : q * 8 + K, :]
            for v in range(NV):
                total = sum_pairs(tiles_ref[p, q, v].astype(jnp.float32) * inputs)
                for n in range(2 * BLK // LANES):
                    at = v * CB * K + q * K
                    partial[n, at : at + K, :] = total[:, n * LANES : (n + 1) * LANES]
        for v in range(NV):
            lanes = slice(v * BLK, (v + 1) * BLK)
            total = None
            for k in range(K):
                rows = pl.ds(v * CB * K + k, CB, stride=K)
                one = jnp.concatenate([partial[n, rows, :] for n in range(2 * BLK // LANES)], axis=1)
                total = one if total is None else total + one
            out_ref[p, :, lanes] = source_ref[p, :, lanes] - fold_pair(total)
        return carry

    lax.fori_loop(0, SB, block_row, 0)


def finish(base_ref, spectral_ref, state_ref, inverse_ref, coef_ref, dst_ref, residual_ref, next_ref, lagged):
    coef = coef_ref[...].astype(jnp.float32)
    spread, cells = [], []
    for side in range(2):
        row = FACE_ROW + side * 16
        pack = jnp.concatenate([spectral_ref[row : row + NV, :], spectral_ref[row + 8 : row + 8 + NV, :]], axis=1)
        contrib = []
        for v in range(NV):
            at = (side * NV + v) * NV
            contrib.append(jnp.sum(coef[at : at + NV] * pack, axis=0, keepdims=True))
        contrib = jnp.concatenate(contrib + [jnp.zeros((8 - NV, PF), jnp.float32)], axis=0)
        block, cell = split_cells(dst_ref[side : side + 1, :])
        spread.append(
            jnp.concatenate([jnp.where(block == b, contrib, 0.0) for b in range(SB * CB)], axis=0)
        )
        cells.append(one_hot(BLK, cell))
    stacked = jnp.concatenate(three_parts(jnp.concatenate(spread, axis=1)), axis=0)
    placed = lax.dot_general(
        stacked,
        jnp.concatenate(cells, axis=1),
        (((1,), (1,)), ((), ())),
        preferred_element_type=jnp.float32,
    )
    count = SB * CB * 8
    put(lagged, 0, count, placed[:count] + (placed[count : 2 * count] + placed[2 * count :]))
    for p in range(SB):
        first = p * STRIPS * 8
        spectral = jnp.concatenate(
            [spectral_ref[first + 8 * n : first + 8 * n + 8, :] for n in range(STRIPS)], axis=1
        )
        residual_ref[p] = base_ref[p] - spectral
        for v in range(NV):
            lanes = slice(v * BLK, (v + 1) * BLK)
            residual_ref[p, :, lanes] = (
                residual_ref[p, :, lanes] - take(lagged, p * CB * 8 + v)
            )

        for v in range(NV):
            lanes = slice(v * BLK, (v + 1) * BLK)
            product = inverse_ref[p, v].astype(jnp.float32) * residual_ref[p]
            next_ref[p, :, lanes] = state_ref[p, :, lanes] + fold_pair(sum_pairs(product))


def middle_kernel(
    base_ref, spectral_ref, state_ref, inverse_ref, coef_ref, dst_ref, src_ref, next_ref, send_ref, low_ref, high_ref, residual_ref, lagged
):
    finish(base_ref, spectral_ref, state_ref, inverse_ref, coef_ref, dst_ref, residual_ref, next_ref, lagged)
    emit_exchange(next_ref, src_ref, send_ref)
    emit_edges(next_ref, low_ref, high_ref)


def last_kernel(
    base_ref, spectral_ref, state_ref, inverse_ref, coef_ref, dst_ref, next_ref, residual_ref, lagged
):
    finish(base_ref, spectral_ref, state_ref, inverse_ref, coef_ref, dst_ref, residual_ref, next_ref, lagged)


def f32(*shape):
    return jax.ShapeDtypeStruct(shape, jnp.float32)


STATE = f32(SB, CB, WIDTH)
EDGE = f32(SB, WIDTH)
SEND = f32(NT * SHARE, LANES)
FINISH_SCRATCH = [
    pltpu.VMEM((3, SB * CB * 8, LANES), jnp.float32),
]
def room(mebibytes):
    return pltpu.CompilerParams(vmem_limit_bytes=mebibytes << 20)


def in_hbm(array):
    return pltpu.with_memory_space_constraint(array, pltpu.HBM)


def start_call(state, src):
    return pl.pallas_call(
        start_kernel,
        out_shape=(SEND, EDGE, EDGE),
        in_specs=[pl.BlockSpec(memory_space=pltpu.HBM)] * 2,
        scratch_shapes=[
            pltpu.VMEM(state.shape, state.dtype),
            pltpu.VMEM(src.shape, src.dtype),
            pltpu.SemaphoreType.DMA((2,)),
        ],
        compiler_params=room(8),
    )(in_hbm(state), in_hbm(src))


def spectral_call(who, received):
    return pl.pallas_call(
        spectral_kernel,
        out_shape=f32(NT, SHARE, LANES),
        in_specs=[pl.BlockSpec(memory_space=pltpu.SMEM), pl.BlockSpec(memory_space=pltpu.VMEM)],
        compiler_params=room(4),
    )(who, received)


def tile_call(cols, tiles, state, left, right, below, above, source):
    in_vmem, raw = pl.BlockSpec(memory_space=pltpu.VMEM), pl.BlockSpec(memory_space=pl.ANY)
    return pl.pallas_call(
        tile_kernel,
        out_shape=STATE,
        in_specs=[raw] * 3 + [in_vmem] * 4 + [raw],
        scratch_shapes=[
            pltpu.SMEM(cols.shape, cols.dtype),
            pltpu.VMEM(tiles.shape, tiles.dtype),
            pltpu.VMEM(source.shape, source.dtype),
            pltpu.VMEM(((SB + 2) * 16, WIDTH), jnp.float32),
            pltpu.VMEM((CB * 8, WIDTH), jnp.float32),
            pltpu.VMEM((2 * BLK // LANES, NV * CB * K, LANES), jnp.float32),
            pltpu.SemaphoreType.DMA((SB + 2,)),
            pltpu.SemaphoreType.DMA((SB,)),
        ],
        compiler_params=room(8),
    )(in_hbm(cols), in_hbm(tiles), state, left, right, below, above, in_hbm(source))


def finish_specs(count):
    return [pl.BlockSpec(memory_space=pltpu.VMEM)] * count


def middle_call(base, spectral, state, inverse, coef, dst, src):
    return pl.pallas_call(
        middle_kernel,
        out_shape=(STATE, SEND, EDGE, EDGE),
        in_specs=finish_specs(7),
        scratch_shapes=[pltpu.VMEM((SB, CB, WIDTH), jnp.float32)] + FINISH_SCRATCH,
        compiler_params=room(8),
    )(base, spectral, state, inverse, coef, dst, src)


def last_call(base, spectral, state, inverse, coef, dst):
    return pl.pallas_call(
        last_kernel,
        out_shape=(STATE, STATE),
        in_specs=finish_specs(6),
        scratch_shapes=FINISH_SCRATCH,
        compiler_params=room(8),
    )(base, spectral, state, inverse, coef, dst)


def exchange(array):
    return lax.all_to_all(array, "inst", 0, 0, tiled=True)


def halos(state, low_edge, high_edge):
    n = lax.axis_size("span")
    below = lax.ppermute(state[SB - 1], "span", [(i, i + 1) for i in range(n - 1)])
    above = lax.ppermute(state[0], "span", [(i + 1, i) for i in range(n - 1)])
    low_edge = jnp.concatenate([low_edge, below[CB - 1 :], above[CB - 1 :]], axis=0)
    high_edge = jnp.concatenate([high_edge, below[:1], above[:1]], axis=0)
    n = lax.axis_size("chord")
    left = lax.ppermute(low_edge, "chord", [(i, (i + 1) % n) for i in range(n)])
    right = lax.ppermute(high_edge, "chord", [(i, (i - 1) % n) for i in range(n)])
    return left, right, below, above


def per_device(adj_source, adj_start, tiles, tile_cols, inverse_diag, face_src, face_dst, lag_coef):
    source, state = adj_source[0], adj_start[0]
    tiles = tiles[0].transpose(0, 1, 3, 2, 4)
    inverse = inverse_diag[0].transpose(0, 2, 1, 3)
    tile_cols = tile_cols.transpose(0, 2, 1)
    coef = lag_coef[0]
    who = lax.axis_index("inst").astype(jnp.int32)[None]
    send, low_edge, high_edge = start_call(state, face_src)
    for sweep in range(SWEEPS):
        received = exchange(send.reshape(NT, SHARE, LANES))
        left, right, below, above = halos(state, low_edge, high_edge)
        spectral = exchange(spectral_call(who, received)).reshape(NT * SHARE, LANES)
        base = tile_call(tile_cols, tiles, in_hbm(state) if sweep == 0 else state, left, right, below, above, source)
        if sweep < SWEEPS - 1:
            state, send, low_edge, high_edge = middle_call(
                base, spectral, state, inverse, coef, face_dst, face_src
            )
        else:
            state, residual = last_call(base, spectral, state, inverse, coef, face_dst)
    return state[None], residual[None]


def solution(mesh):
    return jax.shard_map(
        per_device,
        mesh=mesh,
        in_specs=(
            P("inst", "span", "chord", None),
            P("inst", "span", "chord", None),
            P("inst", "span", "chord", None, None, None),
            P("span", "chord", None),
            P("inst", "span", "chord", None, None),
            P(None, ("span", "chord")),
            P(None, ("span", "chord")),
            P("inst", None, ("span", "chord")),
        ),
        out_specs=(P("inst", "span", "chord", None), P("inst", "span", "chord", None)),
        check_vma=False,
    )
```

```python
import math

import jax
import jax.numpy as jnp
from jax import lax
from jax.experimental import pallas as pl
from jax.experimental.pallas import tpu as pltpu
from jax.sharding import PartitionSpec as P

NV = 6
BLK = 320
SB = 4
CB = 8
K = 4
PF = 256
SWEEPS = 2
NT = 16
LAG = 4
WIDTH = NV * BLK
LANES = 128
STRIPS = WIDTH // LANES
SHARE = 32
FACE_ROW = SB * STRIPS * 8
OWNER = (0, 3, 6, 9, 12, 15, 2, 5, 8, 11, 14, 1, 4, 7, 10, 13)
SLOT = tuple(OWNER.index(t) for t in range(NT))

rotor_rate = 0.25
spectral_viscosity = 0.03


def spectral_coefficients():
    values = []
    for offset in range(NT):
        parity = 1.0 if offset % 2 == 0 else -1.0
        if offset == 0:
            first, second = 0.0, -(NT * NT + 2) / 12.0
        else:
            angle = math.pi * offset / NT
            first = 0.5 * parity * math.cos(angle) / math.sin(angle)
            second = -0.5 * parity / math.sin(angle) ** 2
        values.append(rotor_rate * first - spectral_viscosity * second)
    return values


def split_cells(cells):
    block = lax.shift_right_logical(cells * 6554, 21)
    return block, cells - block * BLK


def three_parts(value):
    high = value.astype(jnp.bfloat16)
    rest = value - high.astype(jnp.float32)
    middle = rest.astype(jnp.bfloat16)
    low = (rest - middle.astype(jnp.float32)).astype(jnp.bfloat16)
    return high, middle, low


def one_hot(size, row):
    hit = lax.broadcasted_iota(jnp.int32, (size, row.shape[1]), 0) == row
    return jnp.where(hit, 1.0, 0.0).astype(jnp.bfloat16)


def emit_exchange(state_ref, src_ref, send_ref):
    for p in range(SB):
        for strip in range(STRIPS):
            row = (p * STRIPS + strip) * 8
            send_ref[row : row + 8, :] = state_ref[p, :, strip * LANES : (strip + 1) * LANES]
    flat = [
        jnp.concatenate([state_ref[p, :, w * BLK : (w + 1) * BLK] for p in range(SB)], axis=0)
        for w in range(NV)
    ]
    rows = SB * CB
    parts = [three_parts(value) for value in flat]
    stacked = jnp.concatenate([parts[w][n] for n in range(3) for w in range(NV)], axis=0)
    for side in range(2):
        block, cell = split_cells(src_ref[side : side + 1, :])
        picked = jnp.dot(stacked, one_hot(BLK, cell), preferred_element_type=jnp.float32)
        count = NV * rows
        picked = picked[:count] + (picked[count : 2 * count] + picked[2 * count :])
        mine = lax.broadcasted_iota(jnp.int32, (rows, PF), 0) == block
        pack = jnp.concatenate(
            [
                jnp.sum(jnp.where(mine, picked[w * rows : (w + 1) * rows], 0.0), axis=0, keepdims=True)
                for w in range(NV)
            ]
            + [jnp.zeros((8 - NV, PF), jnp.float32)],
            axis=0,
        )
        for half in range(2):
            row = FACE_ROW + side * 16 + half * 8
            send_ref[row : row + 8, :] = pack[:, half * LANES : (half + 1) * LANES]


def emit_edges(state_ref, low_ref, high_ref):
    for p in range(SB):
        low_ref[p : p + 1, :] = state_ref[p, CB - 1 : CB, :]
        high_ref[p : p + 1, :] = state_ref[p, 0:1, :]


def start_kernel(state_ref, src_ref, send_ref, low_ref, high_ref, state, src, sems):
    copies = [
        pltpu.make_async_copy(state_ref, state, sems.at[0]),
        pltpu.make_async_copy(src_ref, src, sems.at[1]),
    ]
    for copy in copies:
        copy.start()
    for copy in copies:
        copy.wait()
    emit_exchange(state, src, send_ref)
    emit_edges(state, low_ref, high_ref)


def spectral_kernel(who_ref, in_ref, out_ref):
    coef = spectral_coefficients()
    half = NT // 2

    @pl.when(who_ref[0] != OWNER[NT - 1])
    def _():
        for group in range(SHARE // 8):
            rows = slice(group * 8, group * 8 + 8)
            sums = [in_ref[SLOT[s], rows, :] + in_ref[SLOT[s + half], rows, :] for s in range(half)]
            gaps = [in_ref[SLOT[s], rows, :] - in_ref[SLOT[s + half], rows, :] for s in range(half)]
            for t in range(half):
                even = odd = None
                for s in range(half):
                    near, far = coef[(s - t) % NT], coef[(s - t + half) % NT]
                    one = sums[s] * jnp.float32(0.5 * (near + far))
                    two = gaps[s] * jnp.float32(0.5 * (near - far))
                    even = one if even is None else even + one
                    odd = two if odd is None else odd + two
                out_ref[SLOT[t], rows, :] = even + odd
                out_ref[SLOT[t + half], rows, :] = even - odd

    @pl.when(who_ref[0] == OWNER[NT - 1])
    def _():
        for t in range(NT):
            out_ref[SLOT[t], 0:16, :] = in_ref[SLOT[(t - LAG) % NT], 0:16, :]
            out_ref[SLOT[t], 16:32, :] = in_ref[SLOT[(t + LAG) % NT], 16:32, :]


def put(ref, row, count, value):
    ref[0, pl.ds(row, count), :] = value[:, :LANES]
    ref[1, pl.ds(row, count), :] = value[:, LANES : 2 * LANES]
    ref[2, pl.ds(row, count), 0 : BLK - 2 * LANES] = value[:, 2 * LANES :]


def take(ref, row):
    parts = [ref[n, pl.ds(row, CB, stride=8), :] for n in range(3)]
    return jnp.concatenate(parts, axis=1)[:, :BLK]


def fold_pair(total):
    return total[:, :BLK] + total[:, BLK:]


def sum_pairs(product):
    pair = 2 * BLK
    return product[:, :pair] + product[:, pair : 2 * pair] + product[:, 2 * pair :]


def choose(cols_ref, p, q, wide, chosen):
    for k in range(K):
        code = cols_ref[p, k, q]
        a = lax.shift_right_logical(code * 11, 5)
        side = q + code - 3 * a - 1
        column = jnp.where(side < 0, CB, jnp.where(side == CB, CB + 1, side))
        row = (p + a) * 16 + column
        chosen[q * 8 + k : q * 8 + k + 1, :] = wide[pl.ds(row, 1), :]
    return chosen[q * 8 : q * 8 + K, :]


def weigh(tile_ref, inputs, partial, q):
    for v in range(NV):
        total = sum_pairs(tile_ref[v].astype(jnp.float32) * inputs)
        for n in range(2 * BLK // LANES):
            row = v * CB * K + q * K
            partial[n, row : row + K, :] = total[:, n * LANES : (n + 1) * LANES]


def sum_slots(partial, v):
    total = None
    for k in range(K):
        rows = pl.ds(v * CB * K + k, CB, stride=K)
        one = jnp.concatenate([partial[n, rows, :] for n in range(2 * BLK // LANES)], axis=1)
        total = one if total is None else total + one
    return fold_pair(total)


def inner_kernel(cols_hbm, tiles_hbm, state_ref, out_ref, cols_ref, tiles_ref, wide, chosen, partial, sems, tile_sems):
    def fetch(p):
        return pltpu.make_async_copy(
            tiles_hbm.at[p, pl.ds(1, CB - 2)], tiles_ref.at[p], tile_sems.at[p]
        )

    copies = [pltpu.make_async_copy(cols_hbm, cols_ref, sems.at[0])]
    for row in range(SB):
        base = (row + 1) * 16
        copies.append(
            pltpu.make_async_copy(state_ref.at[row], wide.at[pl.ds(base, CB)], sems.at[row + 1])
        )
    for copy in copies:
        copy.start()
    for p in range(1, SB - 1):
        fetch(p).start()
    partial[...] = jnp.zeros(partial.shape, jnp.float32)
    for copy in copies:
        copy.wait()

    def block_row(p, carry):
        fetch(p).wait()
        for q in range(1, CB - 1):
            weigh(tiles_ref.at[p, q - 1], choose(cols_ref, p, q, wide, chosen), partial, q)
        for v in range(NV):
            out_ref[p - 1, :, v * BLK : (v + 1) * BLK] = sum_slots(partial, v)
        return carry

    lax.fori_loop(1, SB - 1, block_row, 0)


def outer_kernel(
    cols_hbm, tiles_hbm, state_ref, left_ref, right_ref, below_ref, above_ref, source_hbm, inner_ref, out_ref, cols_ref, rows_ref, ends_ref, source_ref, wide, chosen, partial, sems, row_sems, end_sems
):
    def fetch(p, slot):
        return pltpu.make_async_copy(tiles_hbm.at[p], rows_ref.at[slot], row_sems.at[slot])

    def fetch_end(n):
        p, q = 1 + n // 2, (n % 2) * (CB - 1)
        return pltpu.make_async_copy(tiles_hbm.at[p, q], ends_ref.at[n], end_sems.at[n])

    copies = [pltpu.make_async_copy(cols_hbm, cols_ref, sems.at[0])]
    for row in range(SB):
        base = (row + 1) * 16
        copies.append(
            pltpu.make_async_copy(state_ref.at[row], wide.at[pl.ds(base, CB)], sems.at[row + 1])
        )
    copies.append(pltpu.make_async_copy(source_hbm, source_ref, sems.at[SB + 1]))
    for copy in copies:
        copy.start()
    for n in range(2 * (SB - 2)):
        fetch_end(n).start()
    for slot in range(2):
        fetch(slot * (SB - 1), slot).start()
    wide[0:CB, :] = below_ref[...]
    wide[(SB + 1) * 16 : (SB + 1) * 16 + CB, :] = above_ref[...]
    for row, base in enumerate([16, 32, 48, 64, 0, (SB + 1) * 16]):
        wide[base + 8 : base + 9, :] = left_ref[row : row + 1, :]
        wide[base + 9 : base + 10, :] = right_ref[row : row + 1, :]
    partial[...] = jnp.zeros(partial.shape, jnp.float32)
    for copy in copies:
        copy.wait()
    for p in range(1, SB - 1):
        for end in range(2):
            n, q = 2 * (p - 1) + end, end * (CB - 1)
            fetch_end(n).wait()
            weigh(ends_ref.at[n], choose(cols_ref, p, q, wide, chosen), partial, q)
        for v in range(NV):
            lanes = slice(v * BLK, (v + 1) * BLK)
            out_ref[p, :, lanes] = source_ref[p, :, lanes] - (inner_ref[p - 1, :, lanes] + sum_slots(partial, v))

    def block_row(slot, carry):
        p = slot * (SB - 1)
        fetch(p, slot).wait()
        for q in range(CB):
            weigh(rows_ref.at[slot, q], choose(cols_ref, p, q, wide, chosen), partial, q)
        for v in range(NV):
            lanes = slice(v * BLK, (v + 1) * BLK)
            out_ref[p, :, lanes] = source_ref[p, :, lanes] - sum_slots(partial, v)
        return carry

    lax.fori_loop(0, 2, block_row, 0)


def finish(base_ref, spectral_ref, state_ref, inverse_ref, coef_ref, dst_ref, residual_ref, next_ref, lagged):
    coef = coef_ref[...].astype(jnp.float32)
    spread, cells = [], []
    for side in range(2):
        row = FACE_ROW + side * 16
        pack = jnp.concatenate([spectral_ref[row : row + NV, :], spectral_ref[row + 8 : row + 8 + NV, :]], axis=1)
        contrib = []
        for v in range(NV):
            at = (side * NV + v) * NV
            contrib.append(jnp.sum(coef[at : at + NV] * pack, axis=0, keepdims=True))
        contrib = jnp.concatenate(contrib + [jnp.zeros((8 - NV, PF), jnp.float32)], axis=0)
        block, cell = split_cells(dst_ref[side : side + 1, :])
        spread.append(
            jnp.concatenate([jnp.where(block == b, contrib, 0.0) for b in range(SB * CB)], axis=0)
        )
        cells.append(one_hot(BLK, cell))
    stacked = jnp.concatenate(three_parts(jnp.concatenate(spread, axis=1)), axis=0)
    placed = lax.dot_general(
        stacked,
        jnp.concatenate(cells, axis=1),
        (((1,), (1,)), ((), ())),
        preferred_element_type=jnp.float32,
    )
    count = SB * CB * 8
    put(lagged, 0, count, placed[:count] + (placed[count : 2 * count] + placed[2 * count :]))
    for p in range(SB):
        first = p * STRIPS * 8
        spectral = jnp.concatenate(
            [spectral_ref[first + 8 * n : first + 8 * n + 8, :] for n in range(STRIPS)], axis=1
        )
        residual_ref[p] = base_ref[p] - spectral
        for v in range(NV):
            lanes = slice(v * BLK, (v + 1) * BLK)
            residual_ref[p, :, lanes] = (
                residual_ref[p, :, lanes] - take(lagged, p * CB * 8 + v)
            )

        for v in range(NV):
            lanes = slice(v * BLK, (v + 1) * BLK)
            product = inverse_ref[p, v].astype(jnp.float32) * residual_ref[p]
            next_ref[p, :, lanes] = state_ref[p, :, lanes] + fold_pair(sum_pairs(product))


def middle_kernel(
    base_ref, spectral_ref, state_ref, inverse_ref, coef_ref, dst_ref, src_ref, next_ref, send_ref, low_ref, high_ref, residual_ref, lagged
):
    finish(base_ref, spectral_ref, state_ref, inverse_ref, coef_ref, dst_ref, residual_ref, next_ref, lagged)
    emit_exchange(next_ref, src_ref, send_ref)
    emit_edges(next_ref, low_ref, high_ref)


def last_kernel(
    base_ref, spectral_ref, state_ref, inverse_ref, coef_ref, dst_ref, next_ref, residual_ref, lagged
):
    finish(base_ref, spectral_ref, state_ref, inverse_ref, coef_ref, dst_ref, residual_ref, next_ref, lagged)


def f32(*shape):
    return jax.ShapeDtypeStruct(shape, jnp.float32)


STATE = f32(SB, CB, WIDTH)
EDGE = f32(SB, WIDTH)
SEND = f32(NT * SHARE, LANES)
FINISH_SCRATCH = [
    pltpu.VMEM((3, SB * CB * 8, LANES), jnp.float32),
]
def room(mebibytes):
    return pltpu.CompilerParams(vmem_limit_bytes=mebibytes << 20)


def in_hbm(array):
    return pltpu.with_memory_space_constraint(array, pltpu.HBM)


def start_call(state, src):
    return pl.pallas_call(
        start_kernel,
        out_shape=(SEND, EDGE, EDGE),
        in_specs=[pl.BlockSpec(memory_space=pltpu.HBM)] * 2,
        scratch_shapes=[
            pltpu.VMEM(state.shape, state.dtype),
            pltpu.VMEM(src.shape, src.dtype),
            pltpu.SemaphoreType.DMA((2,)),
        ],
        compiler_params=room(8),
    )(in_hbm(state), in_hbm(src))


def spectral_call(who, received):
    return pl.pallas_call(
        spectral_kernel,
        out_shape=f32(NT, SHARE, LANES),
        in_specs=[pl.BlockSpec(memory_space=pltpu.SMEM), pl.BlockSpec(memory_space=pltpu.VMEM)],
        compiler_params=room(4),
    )(who, received)


TILE_SCRATCH = [
    pltpu.VMEM(((SB + 2) * 16, WIDTH), jnp.float32),
    pltpu.VMEM((CB * 8, WIDTH), jnp.float32),
    pltpu.VMEM((2 * BLK // LANES, NV * CB * K, LANES), jnp.float32),
    pltpu.SemaphoreType.DMA((SB + 2,)),
]


def inner_call(cols, tiles, state):
    return pl.pallas_call(
        inner_kernel,
        out_shape=f32(SB - 2, CB, WIDTH),
        in_specs=[pl.BlockSpec(memory_space=pl.ANY)] * 3,
        scratch_shapes=[
            pltpu.SMEM(cols.shape, cols.dtype),
            pltpu.VMEM((SB, CB - 2, *tiles.shape[2:]), tiles.dtype),
            *TILE_SCRATCH,
            pltpu.SemaphoreType.DMA((SB,)),
        ],
        compiler_params=room(8),
    )(in_hbm(cols), in_hbm(tiles), state)


def outer_call(cols, tiles, state, left, right, below, above, source, inner):
    in_vmem, raw = pl.BlockSpec(memory_space=pltpu.VMEM), pl.BlockSpec(memory_space=pl.ANY)
    return pl.pallas_call(
        outer_kernel,
        out_shape=STATE,
        in_specs=[raw] * 3 + [in_vmem] * 4 + [raw, in_vmem],
        scratch_shapes=[
            pltpu.SMEM(cols.shape, cols.dtype),
            pltpu.VMEM((2, *tiles.shape[1:]), tiles.dtype),
            pltpu.VMEM((2 * (SB - 2), *tiles.shape[2:]), tiles.dtype),
            pltpu.VMEM(source.shape, source.dtype),
            *TILE_SCRATCH,
            pltpu.SemaphoreType.DMA((2,)),
            pltpu.SemaphoreType.DMA((2 * (SB - 2),)),
        ],
        compiler_params=room(8),
    )(in_hbm(cols), in_hbm(tiles), state, left, right, below, above, in_hbm(source), inner)


def finish_specs(count):
    return [pl.BlockSpec(memory_space=pltpu.VMEM)] * count


def middle_call(base, spectral, state, inverse, coef, dst, src):
    return pl.pallas_call(
        middle_kernel,
        out_shape=(STATE, SEND, EDGE, EDGE),
        in_specs=finish_specs(7),
        scratch_shapes=[pltpu.VMEM((SB, CB, WIDTH), jnp.float32)] + FINISH_SCRATCH,
        compiler_params=room(8),
    )(base, spectral, state, inverse, coef, dst, src)


def last_call(base, spectral, state, inverse, coef, dst):
    return pl.pallas_call(
        last_kernel,
        out_shape=(STATE, STATE),
        in_specs=finish_specs(6),
        scratch_shapes=FINISH_SCRATCH,
        compiler_params=room(8),
    )(base, spectral, state, inverse, coef, dst)


def exchange(array):
    return lax.all_to_all(array, "inst", 0, 0, tiled=True, axis_index_groups=[list(OWNER)])


def halos(state, low_edge, high_edge):
    n = lax.axis_size("span")
    below = lax.ppermute(state[SB - 1], "span", [(i, i + 1) for i in range(n - 1)])
    above = lax.ppermute(state[0], "span", [(i + 1, i) for i in range(n - 1)])
    low_edge = jnp.concatenate([low_edge, below[CB - 1 :], above[CB - 1 :]], axis=0)
    high_edge = jnp.concatenate([high_edge, below[:1], above[:1]], axis=0)
    n = lax.axis_size("chord")
    left = lax.ppermute(low_edge, "chord", [(i, (i + 1) % n) for i in range(n)])
    right = lax.ppermute(high_edge, "chord", [(i, (i - 1) % n) for i in range(n)])
    return left, right, below, above


def per_device(adj_source, adj_start, tiles, tile_cols, inverse_diag, face_src, face_dst, lag_coef):
    source, state = adj_source[0], adj_start[0]
    tiles = tiles[0].transpose(0, 1, 3, 2, 4)
    inverse = inverse_diag[0].transpose(0, 2, 1, 3)
    tile_cols = tile_cols.transpose(0, 2, 1)
    coef = lag_coef[0]
    who = lax.axis_index("inst").astype(jnp.int32)[None]
    send, low_edge, high_edge = start_call(state, face_src)
    for sweep in range(SWEEPS):
        received = exchange(send.reshape(NT, SHARE, LANES))
        left, right, below, above = halos(state, low_edge, high_edge)
        placed = in_hbm(state) if sweep == 0 else state
        inner = inner_call(tile_cols, tiles, placed)
        received, inner = lax.optimization_barrier((received, inner))
        spectral = exchange(spectral_call(who, received)).reshape(NT * SHARE, LANES)
        base = outer_call(tile_cols, tiles, placed, left, right, below, above, source, inner)
        if sweep < SWEEPS - 1:
            state, send, low_edge, high_edge = middle_call(
                base, spectral, state, inverse, coef, face_dst, face_src
            )
        else:
            state, residual = last_call(base, spectral, state, inverse, coef, face_dst)
    return state[None], residual[None]


def solution(mesh):
    return jax.shard_map(
        per_device,
        mesh=mesh,
        in_specs=(
            P("inst", "span", "chord", None),
            P("inst", "span", "chord", None),
            P("inst", "span", "chord", None, None, None),
            P("span", "chord", None),
            P("inst", "span", "chord", None, None),
            P(None, ("span", "chord")),
            P(None, ("span", "chord")),
            P("inst", None, ("span", "chord")),
        ),
        out_specs=(P("inst", "span", "chord", None), P("inst", "span", "chord", None)),
        check_vma=False,
    )
```

```python
import math

import jax
import jax.numpy as jnp
from jax import lax
from jax.experimental import pallas as pl
from jax.experimental.pallas import tpu as pltpu
from jax.sharding import PartitionSpec as P

NV = 6
BLK = 320
SB = 4
CB = 8
K = 4
PF = 256
SWEEPS = 2
NT = 16
LAG = 4
WIDTH = NV * BLK
LANES = 128
STRIPS = WIDTH // LANES
SHARE = 32
FACE_ROW = SB * STRIPS * 8
OWNER = (0, 3, 6, 9, 12, 15, 2, 5, 8, 11, 14, 1, 4, 7, 10, 13)
SLOT = tuple(OWNER.index(t) for t in range(NT))

rotor_rate = 0.25
spectral_viscosity = 0.03


def spectral_coefficients():
    values = []
    for offset in range(NT):
        parity = 1.0 if offset % 2 == 0 else -1.0
        if offset == 0:
            first, second = 0.0, -(NT * NT + 2) / 12.0
        else:
            angle = math.pi * offset / NT
            first = 0.5 * parity * math.cos(angle) / math.sin(angle)
            second = -0.5 * parity / math.sin(angle) ** 2
        values.append(rotor_rate * first - spectral_viscosity * second)
    return values


def split_cells(cells):
    block = lax.shift_right_logical(cells * 6554, 21)
    return block, cells - block * BLK


def three_parts(value):
    high = value.astype(jnp.bfloat16)
    rest = value - high.astype(jnp.float32)
    middle = rest.astype(jnp.bfloat16)
    low = (rest - middle.astype(jnp.float32)).astype(jnp.bfloat16)
    return high, middle, low


def one_hot(size, row):
    hit = lax.broadcasted_iota(jnp.int32, (size, row.shape[1]), 0) == row
    return jnp.where(hit, 1.0, 0.0).astype(jnp.bfloat16)


def emit_exchange(state_ref, src_ref, send_ref):
    for p in range(SB):
        for strip in range(STRIPS):
            row = (p * STRIPS + strip) * 8
            send_ref[row : row + 8, :] = state_ref[p, :, strip * LANES : (strip + 1) * LANES]
    flat = [
        jnp.concatenate([state_ref[p, :, w * BLK : (w + 1) * BLK] for p in range(SB)], axis=0)
        for w in range(NV)
    ]
    rows = SB * CB
    parts = [three_parts(value) for value in flat]
    stacked = jnp.concatenate([parts[w][n] for n in range(3) for w in range(NV)], axis=0)
    for side in range(2):
        block, cell = split_cells(src_ref[side : side + 1, :])
        picked = jnp.dot(stacked, one_hot(BLK, cell), preferred_element_type=jnp.float32)
        count = NV * rows
        picked = picked[:count] + (picked[count : 2 * count] + picked[2 * count :])
        mine = lax.broadcasted_iota(jnp.int32, (rows, PF), 0) == block
        pack = jnp.concatenate(
            [
                jnp.sum(jnp.where(mine, picked[w * rows : (w + 1) * rows], 0.0), axis=0, keepdims=True)
                for w in range(NV)
            ]
            + [jnp.zeros((8 - NV, PF), jnp.float32)],
            axis=0,
        )
        for half in range(2):
            row = FACE_ROW + side * 16 + half * 8
            send_ref[row : row + 8, :] = pack[:, half * LANES : (half + 1) * LANES]


def emit_edges(state_ref, low_ref, high_ref):
    for p in range(SB):
        low_ref[p : p + 1, :] = state_ref[p, CB - 1 : CB, :]
        high_ref[p : p + 1, :] = state_ref[p, 0:1, :]


def start_kernel(state_ref, src_ref, send_ref, low_ref, high_ref, state, src, sems):
    copies = [
        pltpu.make_async_copy(state_ref, state, sems.at[0]),
        pltpu.make_async_copy(src_ref, src, sems.at[1]),
    ]
    for copy in copies:
        copy.start()
    for copy in copies:
        copy.wait()
    emit_exchange(state, src, send_ref)
    emit_edges(state, low_ref, high_ref)


def spectral_kernel(who_ref, in_ref, out_ref):
    coef = spectral_coefficients()
    half = NT // 2

    @pl.when(who_ref[0] != OWNER[NT - 1])
    def _():
        for group in range(SHARE // 8):
            rows = slice(group * 8, group * 8 + 8)
            sums = [in_ref[SLOT[s], rows, :] + in_ref[SLOT[s + half], rows, :] for s in range(half)]
            gaps = [in_ref[SLOT[s], rows, :] - in_ref[SLOT[s + half], rows, :] for s in range(half)]
            for t in range(half):
                even = odd = None
                for s in range(half):
                    near, far = coef[(s - t) % NT], coef[(s - t + half) % NT]
                    one = sums[s] * jnp.float32(0.5 * (near + far))
                    two = gaps[s] * jnp.float32(0.5 * (near - far))
                    even = one if even is None else even + one
                    odd = two if odd is None else odd + two
                out_ref[SLOT[t], rows, :] = even + odd
                out_ref[SLOT[t + half], rows, :] = even - odd

    @pl.when(who_ref[0] == OWNER[NT - 1])
    def _():
        for t in range(NT):
            out_ref[SLOT[t], 0:16, :] = in_ref[SLOT[(t - LAG) % NT], 0:16, :]
            out_ref[SLOT[t], 16:32, :] = in_ref[SLOT[(t + LAG) % NT], 16:32, :]


def fold_pair(total):
    return total[:, :BLK] + total[:, BLK:]


def sum_pairs(product):
    pair = 2 * BLK
    return product[:, :pair] + product[:, pair : 2 * pair] + product[:, 2 * pair :]


def choose(cols_ref, p, q, wide, chosen):
    for k in range(K):
        code = cols_ref[p, k, q]
        a = lax.shift_right_logical(code * 11, 5)
        side = q + code - 3 * a - 1
        column = jnp.where(side < 0, CB, jnp.where(side == CB, CB + 1, side))
        row = (p + a) * 16 + column
        chosen[q * 8 + k : q * 8 + k + 1, :] = wide[pl.ds(row, 1), :]
    return chosen[q * 8 : q * 8 + K, :]


def weigh(tile_ref, inputs, partial, q):
    for v in range(NV):
        total = sum_pairs(tile_ref[v].astype(jnp.float32) * inputs)
        for n in range(2 * BLK // LANES):
            row = v * CB * K + q * K
            partial[n, row : row + K, :] = total[:, n * LANES : (n + 1) * LANES]


def sum_slots(partial, v):
    total = None
    for k in range(K):
        rows = pl.ds(v * CB * K + k, CB, stride=K)
        one = jnp.concatenate([partial[n, rows, :] for n in range(2 * BLK // LANES)], axis=1)
        total = one if total is None else total + one
    return fold_pair(total)


def inner_kernel(cols_hbm, tiles_hbm, state_ref, out_ref, cols_ref, tiles_ref, wide, chosen, partial, sems, tile_sems):
    def fetch(p):
        return pltpu.make_async_copy(
            tiles_hbm.at[p, pl.ds(1, CB - 2)], tiles_ref.at[p], tile_sems.at[p]
        )

    copies = [pltpu.make_async_copy(cols_hbm, cols_ref, sems.at[0])]
    for row in range(SB):
        base = (row + 1) * 16
        copies.append(
            pltpu.make_async_copy(state_ref.at[row], wide.at[pl.ds(base, CB)], sems.at[row + 1])
        )
    for copy in copies:
        copy.start()
    for p in range(1, SB - 1):
        fetch(p).start()
    partial[...] = jnp.zeros(partial.shape, jnp.float32)
    for copy in copies:
        copy.wait()

    def block_row(p, carry):
        fetch(p).wait()
        for q in range(1, CB - 1):
            weigh(tiles_ref.at[p, q - 1], choose(cols_ref, p, q, wide, chosen), partial, q)
        for v in range(NV):
            out_ref[p - 1, :, v * BLK : (v + 1) * BLK] = sum_slots(partial, v)
        return carry

    lax.fori_loop(1, SB - 1, block_row, 0)


def outer_kernel(
    cols_hbm, tiles_hbm, state_ref, left_ref, right_ref, below_ref, above_ref, source_hbm, inner_ref, out_ref, cols_ref, rows_ref, ends_ref, source_ref, wide, chosen, partial, sems, row_sems, end_sems
):
    def fetch(p, slot):
        return pltpu.make_async_copy(tiles_hbm.at[p], rows_ref.at[slot], row_sems.at[slot])

    def fetch_end(n):
        p, q = 1 + n // 2, (n % 2) * (CB - 1)
        return pltpu.make_async_copy(tiles_hbm.at[p, q], ends_ref.at[n], end_sems.at[n])

    copies = [pltpu.make_async_copy(cols_hbm, cols_ref, sems.at[0])]
    for row in range(SB):
        base = (row + 1) * 16
        copies.append(
            pltpu.make_async_copy(state_ref.at[row], wide.at[pl.ds(base, CB)], sems.at[row + 1])
        )
    copies.append(pltpu.make_async_copy(source_hbm, source_ref, sems.at[SB + 1]))
    for copy in copies:
        copy.start()
    for n in range(2 * (SB - 2)):
        fetch_end(n).start()
    for slot in range(2):
        fetch(slot * (SB - 1), slot).start()
    wide[0:CB, :] = below_ref[...]
    wide[(SB + 1) * 16 : (SB + 1) * 16 + CB, :] = above_ref[...]
    for row, base in enumerate([16, 32, 48, 64, 0, (SB + 1) * 16]):
        wide[base + 8 : base + 9, :] = left_ref[row : row + 1, :]
        wide[base + 9 : base + 10, :] = right_ref[row : row + 1, :]
    partial[...] = jnp.zeros(partial.shape, jnp.float32)
    for copy in copies:
        copy.wait()
    for p in range(1, SB - 1):
        for end in range(2):
            n, q = 2 * (p - 1) + end, end * (CB - 1)
            fetch_end(n).wait()
            weigh(ends_ref.at[n], choose(cols_ref, p, q, wide, chosen), partial, q)
        for v in range(NV):
            lanes = slice(v * BLK, (v + 1) * BLK)
            out_ref[p, :, lanes] = source_ref[p, :, lanes] - (inner_ref[p - 1, :, lanes] + sum_slots(partial, v))

    def block_row(slot, carry):
        p = slot * (SB - 1)
        fetch(p, slot).wait()
        for q in range(CB):
            weigh(rows_ref.at[slot, q], choose(cols_ref, p, q, wide, chosen), partial, q)
        for v in range(NV):
            lanes = slice(v * BLK, (v + 1) * BLK)
            out_ref[p, :, lanes] = source_ref[p, :, lanes] - sum_slots(partial, v)
        return carry

    lax.fori_loop(0, 2, block_row, 0)


def finish(base_ref, spectral_ref, state_ref, inverse_ref, coef_ref, dst_ref, residual_ref, next_ref):
    coef = coef_ref[...].astype(jnp.float32)
    spread, cells = [], []
    blocks = SB * CB
    for side in range(2):
        row = FACE_ROW + side * 16
        pack = jnp.concatenate([spectral_ref[row : row + NV, :], spectral_ref[row + 8 : row + 8 + NV, :]], axis=1)
        block, cell = split_cells(dst_ref[side : side + 1, :])
        mine = lax.broadcasted_iota(jnp.int32, (blocks, PF), 0) == block
        placed = []
        for v in range(NV):
            at = (side * NV + v) * NV
            contrib = jnp.sum(coef[at : at + NV] * pack, axis=0, keepdims=True)
            placed.append(jnp.where(mine, contrib, 0.0))
        spread.append(jnp.concatenate(placed, axis=0))
        cells.append(one_hot(BLK, cell))
    stacked = jnp.concatenate(three_parts(jnp.concatenate(spread, axis=1)), axis=0)
    lag = lax.dot_general(
        stacked,
        jnp.concatenate(cells, axis=1),
        (((1,), (1,)), ((), ())),
        preferred_element_type=jnp.float32,
    )
    count = NV * blocks
    lag = lag[:count] + (lag[count : 2 * count] + lag[2 * count :])
    for p in range(SB):
        first = p * STRIPS * 8
        spectral = jnp.concatenate(
            [spectral_ref[first + 8 * n : first + 8 * n + 8, :] for n in range(STRIPS)], axis=1
        )
        lagged = jnp.concatenate(
            [lag[v * blocks + p * CB : v * blocks + (p + 1) * CB] for v in range(NV)], axis=1
        )
        residual = base_ref[p] - spectral - lagged
        residual_ref[p] = residual
        change = [
            fold_pair(sum_pairs(inverse_ref[p, v].astype(jnp.float32) * residual)) for v in range(NV)
        ]
        next_ref[p] = state_ref[p] + jnp.concatenate(change, axis=1)


def middle_kernel(
    base_ref, spectral_ref, state_ref, inverse_ref, coef_ref, dst_ref, src_ref, next_ref, send_ref, low_ref, high_ref, residual_ref
):
    finish(base_ref, spectral_ref, state_ref, inverse_ref, coef_ref, dst_ref, residual_ref, next_ref)
    emit_exchange(next_ref, src_ref, send_ref)
    emit_edges(next_ref, low_ref, high_ref)


def last_kernel(
    base_ref, spectral_ref, state_ref, inverse_ref, coef_ref, dst_ref, next_ref, residual_ref
):
    finish(base_ref, spectral_ref, state_ref, inverse_ref, coef_ref, dst_ref, residual_ref, next_ref)


def f32(*shape):
    return jax.ShapeDtypeStruct(shape, jnp.float32)


STATE = f32(SB, CB, WIDTH)
EDGE = f32(SB, WIDTH)
SEND = f32(NT * SHARE, LANES)
def room(mebibytes):
    return pltpu.CompilerParams(vmem_limit_bytes=mebibytes << 20)


def in_hbm(array):
    return pltpu.with_memory_space_constraint(array, pltpu.HBM)


def start_call(state, src):
    return pl.pallas_call(
        start_kernel,
        out_shape=(SEND, EDGE, EDGE),
        in_specs=[pl.BlockSpec(memory_space=pltpu.HBM)] * 2,
        scratch_shapes=[
            pltpu.VMEM(state.shape, state.dtype),
            pltpu.VMEM(src.shape, src.dtype),
            pltpu.SemaphoreType.DMA((2,)),
        ],
        compiler_params=room(8),
    )(in_hbm(state), in_hbm(src))


def spectral_call(who, received):
    return pl.pallas_call(
        spectral_kernel,
        out_shape=f32(NT, SHARE, LANES),
        in_specs=[pl.BlockSpec(memory_space=pltpu.SMEM), pl.BlockSpec(memory_space=pltpu.VMEM)],
        compiler_params=room(4),
    )(who, received)


TILE_SCRATCH = [
    pltpu.VMEM(((SB + 2) * 16, WIDTH), jnp.float32),
    pltpu.VMEM((CB * 8, WIDTH), jnp.float32),
    pltpu.VMEM((2 * BLK // LANES, NV * CB * K, LANES), jnp.float32),
    pltpu.SemaphoreType.DMA((SB + 2,)),
]


def inner_call(cols, tiles, state):
    return pl.pallas_call(
        inner_kernel,
        out_shape=f32(SB - 2, CB, WIDTH),
        in_specs=[pl.BlockSpec(memory_space=pl.ANY)] * 3,
        scratch_shapes=[
            pltpu.SMEM(cols.shape, cols.dtype),
            pltpu.VMEM((SB, CB - 2, *tiles.shape[2:]), tiles.dtype),
            *TILE_SCRATCH,
            pltpu.SemaphoreType.DMA((SB,)),
        ],
        compiler_params=room(8),
    )(in_hbm(cols), in_hbm(tiles), state)


def outer_call(cols, tiles, state, left, right, below, above, source, inner):
    in_vmem, raw = pl.BlockSpec(memory_space=pltpu.VMEM), pl.BlockSpec(memory_space=pl.ANY)
    return pl.pallas_call(
        outer_kernel,
        out_shape=STATE,
        in_specs=[raw] * 3 + [in_vmem] * 4 + [raw, in_vmem],
        scratch_shapes=[
            pltpu.SMEM(cols.shape, cols.dtype),
            pltpu.VMEM((2, *tiles.shape[1:]), tiles.dtype),
            pltpu.VMEM((2 * (SB - 2), *tiles.shape[2:]), tiles.dtype),
            pltpu.VMEM(source.shape, source.dtype),
            *TILE_SCRATCH,
            pltpu.SemaphoreType.DMA((2,)),
            pltpu.SemaphoreType.DMA((2 * (SB - 2),)),
        ],
        compiler_params=room(8),
    )(in_hbm(cols), in_hbm(tiles), state, left, right, below, above, in_hbm(source), inner)


def finish_specs(count):
    return [pl.BlockSpec(memory_space=pltpu.VMEM)] * count


def middle_call(base, spectral, state, inverse, coef, dst, src):
    return pl.pallas_call(
        middle_kernel,
        out_shape=(STATE, SEND, EDGE, EDGE),
        in_specs=finish_specs(7),
        scratch_shapes=[pltpu.VMEM((SB, CB, WIDTH), jnp.float32)],
        compiler_params=room(8),
    )(base, spectral, state, inverse, coef, dst, src)


def last_call(base, spectral, state, inverse, coef, dst):
    return pl.pallas_call(
        last_kernel,
        out_shape=(STATE, STATE),
        in_specs=finish_specs(6),
        compiler_params=room(8),
    )(base, spectral, state, inverse, coef, dst)


def exchange(array):
    return lax.all_to_all(array, "inst", 0, 0, tiled=True, axis_index_groups=[list(OWNER)])


def halos(state, low_edge, high_edge):
    n = lax.axis_size("span")
    below = lax.ppermute(state[SB - 1], "span", [(i, i + 1) for i in range(n - 1)])
    above = lax.ppermute(state[0], "span", [(i + 1, i) for i in range(n - 1)])
    low_edge = jnp.concatenate([low_edge, below[CB - 1 :], above[CB - 1 :]], axis=0)
    high_edge = jnp.concatenate([high_edge, below[:1], above[:1]], axis=0)
    n = lax.axis_size("chord")
    left = lax.ppermute(low_edge, "chord", [(i, (i + 1) % n) for i in range(n)])
    right = lax.ppermute(high_edge, "chord", [(i, (i - 1) % n) for i in range(n)])
    return left, right, below, above


def per_device(adj_source, adj_start, tiles, tile_cols, inverse_diag, face_src, face_dst, lag_coef):
    source, state = adj_source[0], adj_start[0]
    tiles = tiles[0].transpose(0, 1, 3, 2, 4)
    inverse = inverse_diag[0].transpose(0, 2, 1, 3)
    tile_cols = tile_cols.transpose(0, 2, 1)
    coef = lag_coef[0]
    who = lax.axis_index("inst").astype(jnp.int32)[None]
    send, low_edge, high_edge = start_call(state, face_src)
    for sweep in range(SWEEPS):
        received = exchange(send.reshape(NT, SHARE, LANES))
        left, right, below, above = halos(state, low_edge, high_edge)
        placed = in_hbm(state) if sweep == 0 else state
        inner = inner_call(tile_cols, tiles, placed)
        received, inner = lax.optimization_barrier((received, inner))
        spectral = exchange(spectral_call(who, received)).reshape(NT * SHARE, LANES)
        base = outer_call(tile_cols, tiles, placed, left, right, below, above, source, inner)
        if sweep < SWEEPS - 1:
            state, send, low_edge, high_edge = middle_call(
                base, spectral, state, inverse, coef, face_dst, face_src
            )
        else:
            state, residual = last_call(base, spectral, state, inverse, coef, face_dst)
    return state[None], residual[None]


def solution(mesh):
    return jax.shard_map(
        per_device,
        mesh=mesh,
        in_specs=(
            P("inst", "span", "chord", None),
            P("inst", "span", "chord", None),
            P("inst", "span", "chord", None, None, None),
            P("span", "chord", None),
            P("inst", "span", "chord", None, None),
            P(None, ("span", "chord")),
            P(None, ("span", "chord")),
            P("inst", None, ("span", "chord")),
        ),
        out_specs=(P("inst", "span", "chord", None), P("inst", "span", "chord", None)),
        check_vma=False,
    )
```
